32 devices in a mesh: seq: 8 (over y, x, core), fsdp: 4 (over z).
Axes of the slice: x: 2, y: 2, z: 4, core: 2. Of those that a mesh axis runs over, the one named last changes fastest.
Arguments:
- hidden_in: bfloat16 [4, 2048, 1024], P('fsdp', 'seq'), may hold values from -6 to 6
- cotangent: bfloat16 [4, 2048, 1024], P('fsdp', 'seq'), may hold values from -6 to 6
- doc_position: int32 [4, 2048], P('fsdp', 'seq'), may hold values from 0 to 2047, as said below
- norm_gains: float32 [2, 1024], P(None, ('seq', 'fsdp')), may hold values from 0.5 to 1.5
- conv_taps: float32 [3, 1024], P(None, ('seq', 'fsdp')), may hold values from -3 to 3
- in_proj: float32 [1024, 3072], P(('seq', 'fsdp')), may hold values from -0.1875 to 0.1875
- out_proj: float32 [1024, 1024], P(('seq', 'fsdp')), may hold values from -0.1875 to 0.1875
- gate_up: float32 [1024, 9216], P(('seq', 'fsdp')), may hold values from -0.1875 to 0.1875
- down_proj: float32 [4608, 1024], P(('seq', 'fsdp')), may hold values from -0.09375 to 0.09375
- first_gains: float32 [2, 1024], P(None, ('seq', 'fsdp')), may hold values from -56 to 56
- first_taps: float32 [3, 1024], P(None, ('seq', 'fsdp')), may hold values from -56 to 56
- first_in: float32 [1024, 3072], P(('seq', 'fsdp')), may hold values from -56 to 56
- first_out: float32 [1024, 1024], P(('seq', 'fsdp')), may hold values from -56 to 56
- first_gate_up: float32 [1024, 9216], P(('seq', 'fsdp')), may hold values from -14 to 14
- first_down: float32 [4608, 1024], P(('seq', 'fsdp')), may hold values from -32 to 32
- second_gains: float32 [2, 1024], P(None, ('seq', 'fsdp')), may hold values from 2.4576 to 24.576
- second_taps: float32 [3, 1024], P(None, ('seq', 'fsdp')), may hold values from 2.4576 to 24.576
- second_in: float32 [1024, 3072], P(('seq', 'fsdp')), may hold values from 2.4576 to 24.576
- second_out: float32 [1024, 1024], P(('seq', 'fsdp')), may hold values from 2.4576 to 24.576
- second_gate_up: float32 [1024, 9216], P(('seq', 'fsdp')), may hold values from 0.16384 to 1.6384
- second_down: float32 [4608, 1024], P(('seq', 'fsdp')), may hold values from 0.8192 to 8.192
Outputs:
- block_out: float32 [4, 2048, 1024], P('fsdp', 'seq')
- grad_hidden: float32 [4, 2048, 1024], P('fsdp', 'seq')
- grad_gains: float32 [2, 1024], P(None, ('seq', 'fsdp'))
- grad_taps: float32 [3, 1024], P(None, ('seq', 'fsdp'))
- grad_in: float32 [1024, 3072], P(('seq', 'fsdp'))
- grad_out: float32 [1024, 1024], P(('seq', 'fsdp'))
- grad_gate_up: float32 [1024, 9216], P(('seq', 'fsdp'))
- grad_down: float32 [4608, 1024], P(('seq', 'fsdp'))
- new_gains: float32 [2, 1024], P(None, ('seq', 'fsdp'))
- new_taps: float32 [3, 1024], P(None, ('seq', 'fsdp'))
- new_in: float32 [1024, 3072], P(('seq', 'fsdp'))
- new_out: float32 [1024, 1024], P(('seq', 'fsdp'))
- new_gate_up: float32 [1024, 9216], P(('seq', 'fsdp'))
- new_down: float32 [4608, 1024], P(('seq', 'fsdp'))
- next_first_gains: float32 [2, 1024], P(None, ('seq', 'fsdp'))
- next_first_taps: float32 [3, 1024], P(None, ('seq', 'fsdp'))
- next_first_in: float32 [1024, 3072], P(('seq', 'fsdp'))
- next_first_out: float32 [1024, 1024], P(('seq', 'fsdp'))
- next_first_gate_up: float32 [1024, 9216], P(('seq', 'fsdp'))
- next_first_down: float32 [4608, 1024], P(('seq', 'fsdp'))
- next_second_gains: float32 [2, 1024], P(None, ('seq', 'fsdp'))
- next_second_taps: float32 [3, 1024], P(None, ('seq', 'fsdp'))
- next_second_in: float32 [1024, 3072], P(('seq', 'fsdp'))
- next_second_out: float32 [1024, 1024], P(('seq', 'fsdp'))
- next_second_gate_up: float32 [1024, 9216], P(('seq', 'fsdp'))
- next_second_down: float32 [4608, 1024], P(('seq', 'fsdp'))
The draws below stay inside these ranges and needn't reach their ends.
Inputs may be any that keep to these rules, and one draw needn't show every extreme that they name: doc_position[s, t] is 0 where a packed document starts (always at t = 0) and doc_position[s, t - 1] + 1 elsewhere; sequence 0 holds a single document.
All inputs are finite; a program needn't handle non-finite values.
Results may differ from the reference program's by a relative error of at most 0.012.
The reference program's roundings to bfloat16 on the way (of `normed_one`, `gated_input`, `mixer_act`, `normed_two`, `ffn_act`, `grad_both`, `resid_cast` and `grad_proj`) count: a program that leaves them out, or rounds other values in their place, can miss the bound.
Values may be sent and summed in bfloat16 or wider, within the bound.
A program may use at most 256 MiB of HBM per device.

```python
import math
import jax
import jax.numpy as jnp
from jax import lax

D = 1024
FF = 4608
STEP = 3
SEQS = 4
LEN = 2048
TOKENS = 8192


def draw_doc_position(key, part):
    marks = jax.random.randint(key, (SEQS, LEN), 0, 32)
    places = jnp.broadcast_to(jnp.arange(LEN, dtype=jnp.int32), (SEQS, LEN))
    row_ids = jnp.broadcast_to(jnp.arange(SEQS, dtype=jnp.int32)[:, None], (SEQS, LEN))
    starts = jnp.logical_or(jnp.logical_and(marks == 0, row_ids > 0), places == 0)
    latest = lax.cummax(jnp.where(starts, places, 0), axis=1)
    return (places - latest).astype(jnp.int32)


def block_scale(stream_key, dims, split, low, top_value):
    def one(position, blocks):
        draws = jax.random.uniform(jax.random.fold_in(jax.random.fold_in(stream_key, 6), position), (blocks,), jnp.float32, low / len(split), top_value / len(split))
        return jnp.repeat(jnp.exp(draws), dims[position] // blocks).reshape((-1,) + (1,) * (len(dims) - position - 1))

    loudness = one(*split[0])
    for cut in split[1:]:
        loudness = loudness * one(*cut)
    return loudness


def centred(own_key, shape, scale, most, pieces=(), kind=jnp.bfloat16):
    values = scale * jax.random.normal(own_key, shape, jnp.float32)
    if pieces:
        values = values * block_scale(own_key, shape, pieces, -0.22, 0.18)
    return jnp.clip(values, -most, most).astype(kind)


def setup_inputs(seed: int = 0) -> dict:
    splits = jax.random.split(jax.random.key(seed), 22)
    return {
        "hidden_in": centred(splits[0], (SEQS, LEN, D), 1.0, 6.0, ((0, 4), (1, 8))),
        "cotangent": centred(splits[1], (SEQS, LEN, D), 1.0, 6.0, ((0, 4), (1, 8))),
        "doc_position": draw_doc_position(jax.random.fold_in(splits[21], 71), 0),
        "norm_gains": jnp.clip(1.0 + 0.1 * jax.random.normal(splits[3], (2, D), jnp.float32), 0.5, 1.5),
        "conv_taps": centred(splits[4], (3, D), 0.5, 3.0, ((1, 32),), jnp.float32),
        "in_proj": centred(splits[5], (D, 3 * D), D ** -0.5, 0.1875, ((0, 32),), jnp.float32),
        "out_proj": centred(splits[6], (D, D), D ** -0.5, 0.1875, ((0, 32),), jnp.float32),
        "gate_up": centred(splits[7], (D, 2 * FF), D ** -0.5, 0.1875, ((0, 32),), jnp.float32),
        "down_proj": centred(splits[8], (FF, D), FF ** -0.5, 0.09375, ((0, 32),), jnp.float32),
        "first_gains": centred(splits[9], (2, D), (0.1 * TOKENS ** 0.5), 56.0, ((1, 32),), jnp.float32),
        "first_taps": centred(splits[10], (3, D), (0.1 * TOKENS ** 0.5), 56.0, ((1, 32),), jnp.float32),
        "first_in": centred(splits[11], (D, 3 * D), (0.1 * TOKENS ** 0.5), 56.0, ((0, 32),), jnp.float32),
        "first_out": centred(splits[12], (D, D), (0.1 * TOKENS ** 0.5), 56.0, ((0, 32),), jnp.float32),
        "first_gate_up": centred(splits[13], (D, 2 * FF), (0.025 * TOKENS ** 0.5), 14.0, ((0, 32),), jnp.float32),
        "first_down": centred(splits[14], (FF, D), (0.06 * TOKENS ** 0.5), 32.0, ((0, 32),), jnp.float32),
        "second_gains": jnp.clip(jnp.exp(math.log(24.576) - 2.3025851 * jax.random.uniform(splits[15], (2, D), jnp.float32) ** block_scale(splits[15], (2, D), ((1, 32),), -0.2, 0.2)), 2.4576, 24.576),
        "second_taps": jnp.clip(jnp.exp(math.log(24.576) - 2.3025851 * jax.random.uniform(splits[16], (3, D), jnp.float32) ** block_scale(splits[16], (3, D), ((1, 32),), -0.2, 0.2)), 2.4576, 24.576),
        "second_in": jnp.clip(jnp.exp(math.log(24.576) - 2.3025851 * jax.random.uniform(splits[17], (D, 3 * D), jnp.float32) ** block_scale(splits[17], (D, 3 * D), ((0, 32),), -0.2, 0.2)), 2.4576, 24.576),
        "second_out": jnp.clip(jnp.exp(math.log(24.576) - 2.3025851 * jax.random.uniform(splits[18], (D, D), jnp.float32) ** block_scale(splits[18], (D, D), ((0, 32),), -0.2, 0.2)), 2.4576, 24.576),
        "second_gate_up": jnp.clip(jnp.exp(math.log(1.6384) - 2.3025851 * jax.random.uniform(splits[19], (D, 2 * FF), jnp.float32) ** block_scale(splits[19], (D, 2 * FF), ((0, 32),), -0.2, 0.2)), 0.16384, 1.6384),
        "second_down": jnp.clip(jnp.exp(math.log(8.192) - 2.3025852 * jax.random.uniform(splits[20], (FF, D), jnp.float32) ** block_scale(splits[20], (FF, D), ((0, 32),), -0.2, 0.2)), 0.8192, 8.192),
    }


NORM_EPS = 1e-05
BETA_ONE = 0.9
BETA_TWO = 0.999
ADAM_EPS = 1e-08
RATE_MATRIX = 0.005
RATE_VECTOR = 0.2
DECAY = 0.1

def matmul(left, right):
    return jnp.dot(left, right, preferred_element_type=jnp.float32)

def matmul_tn(left, right):
    return lax.dot_general(left, right, (((0,), (0,)), ((), ())), preferred_element_type=jnp.float32)

def matmul_nt(left, right):
    return lax.dot_general(left, right, (((1,), (1,)), ((), ())), preferred_element_type=jnp.float32)

def inverse_rms(values):
    return lax.rsqrt(lax.optimization_barrier(jnp.mean(values * values, axis=-1, keepdims=True)) + NORM_EPS)

def norm_backward(values, scale, gain, grad_normed):
    weighted = grad_normed * gain
    grad_gain = lax.optimization_barrier(jnp.sum(grad_normed * values * scale, axis=0))
    cubed = scale * scale * scale
    grad_values = scale * weighted - values * cubed * lax.optimization_barrier(jnp.mean(weighted * values, axis=-1, keepdims=True))
    return (grad_values, grad_gain)

def adamw_update(param, grad, first, second, rate, decay):
    first_new = BETA_ONE * first + (1.0 - BETA_ONE) * grad
    second_new = BETA_TWO * second + (1.0 - BETA_TWO) * grad * grad
    first_hat = first_new / (1.0 - BETA_ONE ** STEP)
    second_hat = second_new / (1.0 - BETA_TWO ** STEP)
    param_new = param - rate * (first_hat / (jnp.sqrt(second_hat) + ADAM_EPS) + decay * param)
    return (param_new, first_new, second_new)

def shift_down(values, amount):
    padding = jnp.zeros((amount, values.shape[1]), values.dtype)
    return jnp.concatenate([padding, values[:values.shape[0] - amount]], axis=0)

def shift_up(values, amount):
    padding = jnp.zeros((amount, values.shape[1]), values.dtype)
    return jnp.concatenate([values[amount:], padding], axis=0)

def one_row(params_b, row_in, row_cot, row_pos):
    gains_f = params_b[0].astype(jnp.float32)
    taps_f = params_b[1].astype(jnp.float32)
    in_b = params_b[2]
    out_b = params_b[3]
    gate_up_b = params_b[4]
    down_b = params_b[5]
    width = row_in.shape[1]
    hidden_units = gate_up_b.shape[1] // 2
    resid_one = row_in.astype(jnp.float32)
    scale_one = inverse_rms(resid_one)
    normed_one = (resid_one * scale_one * gains_f[0]).astype(jnp.bfloat16)
    projected = matmul(normed_one, in_b)
    b_branch = projected[:, :width]
    c_branch = projected[:, width:2 * width]
    x_branch = projected[:, 2 * width:]
    gated_input = (b_branch * x_branch).astype(jnp.bfloat16)
    gated_f = gated_input.astype(jnp.float32)
    mask_one = (row_pos >= 1).astype(jnp.float32)[:, None]
    mask_two = (row_pos >= 2).astype(jnp.float32)[:, None]
    prev_one = shift_down(gated_f, 1)
    prev_two = shift_down(gated_f, 2)
    conv_out = taps_f[0] * gated_f + mask_one * taps_f[1] * prev_one + mask_two * taps_f[2] * prev_two
    mixer_act = (c_branch * conv_out).astype(jnp.bfloat16)
    resid_two = resid_one + matmul(mixer_act, out_b)
    scale_two = inverse_rms(resid_two)
    normed_two = (resid_two * scale_two * gains_f[1]).astype(jnp.bfloat16)
    ffn_pre = matmul(normed_two, gate_up_b)
    gate_pre = ffn_pre[:, :hidden_units]
    up_pre = ffn_pre[:, hidden_units:]
    sigmoid_gate = jax.nn.sigmoid(gate_pre)
    silu_gate = gate_pre * sigmoid_gate
    ffn_act = (silu_gate * up_pre).astype(jnp.bfloat16)
    block_out = resid_two + matmul(ffn_act, down_b)
    grad_down = matmul_tn(ffn_act, row_cot)
    grad_act = matmul_nt(row_cot, down_b)
    grad_gate = grad_act * up_pre * sigmoid_gate * (1.0 + gate_pre * (1.0 - sigmoid_gate))
    grad_both = jnp.concatenate([grad_gate, grad_act * silu_gate], axis=1).astype(jnp.bfloat16)
    grad_gate_up = matmul_tn(normed_two, grad_both)
    grad_normed = matmul_nt(grad_both, gate_up_b)
    norm_part, gain_two_grad = norm_backward(resid_two, scale_two, gains_f[1], grad_normed)
    grad_resid = row_cot.astype(jnp.float32) + norm_part
    resid_cast = grad_resid.astype(jnp.bfloat16)
    grad_out = matmul_tn(mixer_act, resid_cast)
    grad_mixer = matmul_nt(resid_cast, out_b)
    grad_cbranch = grad_mixer * conv_out
    grad_conv = grad_mixer * c_branch
    masked_one = mask_one * grad_conv
    masked_two = mask_two * grad_conv
    grad_taps = jnp.stack([lax.optimization_barrier(jnp.sum(grad_conv * gated_f, axis=0)), lax.optimization_barrier(jnp.sum(masked_one * prev_one, axis=0)), lax.optimization_barrier(jnp.sum(masked_two * prev_two, axis=0))])
    grad_gated = taps_f[0] * grad_conv + taps_f[1] * shift_up(masked_one, 1) + taps_f[2] * shift_up(masked_two, 2)
    grad_proj = jnp.concatenate([grad_gated * x_branch, grad_cbranch, grad_gated * b_branch], axis=1).astype(jnp.bfloat16)
    grad_in = matmul_tn(normed_one, grad_proj)
    grad_normone = matmul_nt(grad_proj, in_b)
    first_part, gain_one_grad = norm_backward(resid_one, scale_one, gains_f[0], grad_normone)
    grad_hidden = grad_resid + first_part
    grad_gains = jnp.stack([gain_one_grad, gain_two_grad])
    row_grads = (grad_gains, grad_taps, grad_in, grad_out, grad_gate_up, grad_down)
    return (block_out, grad_hidden, row_grads)

def reference(hidden_in, cotangent, doc_position, norm_gains, conv_taps, in_proj, out_proj, gate_up, down_proj, first_gains, first_taps, first_in, first_out, first_gate_up, first_down, second_gains, second_taps, second_in, second_out, second_gate_up, second_down):
    params = (norm_gains, conv_taps, in_proj, out_proj, gate_up, down_proj)
    firsts = (first_gains, first_taps, first_in, first_out, first_gate_up, first_down)
    seconds = (second_gains, second_taps, second_in, second_out, second_gate_up, second_down)
    params_b = tuple((param.astype(jnp.bfloat16) for param in params))
    zero_grads = tuple((jnp.zeros(param.shape, jnp.float32) for param in params))

    def step_rows(totals, row_items):
        row_in, row_cot, row_pos = row_items
        row_out, row_grad, row_grads = one_row(params_b, row_in, row_cot, row_pos)
        summed = tuple((running + extra for running, extra in zip(totals, row_grads)))
        return (summed, (row_out, row_grad))
    totals, outputs = lax.scan(step_rows, zero_grads, (hidden_in, cotangent, doc_position))
    block_out, grad_hidden = outputs
    rates = (RATE_VECTOR, RATE_VECTOR, RATE_MATRIX, RATE_MATRIX, RATE_MATRIX, RATE_MATRIX)
    decays = (0.0, 0.0, DECAY, DECAY, DECAY, DECAY)
    updated = [adamw_update(params[index], totals[index], firsts[index], seconds[index], rates[index], decays[index]) for index in range(6)]
    return (block_out, grad_hidden, totals[0], totals[1], totals[2], totals[3], totals[4], totals[5], updated[0][0], updated[1][0], updated[2][0], updated[3][0], updated[4][0], updated[5][0], updated[0][1], updated[1][1], updated[2][1], updated[3][1], updated[4][1], updated[5][1], updated[0][2], updated[1][2], updated[2][2], updated[3][2], updated[4][2], updated[5][2])
```

```python
import jax
import jax.numpy as jnp
from jax import lax
from jax.sharding import PartitionSpec as P

STEP = 3


NORM_EPS = 1e-05
BETA_ONE = 0.9
BETA_TWO = 0.999
ADAM_EPS = 1e-08
RATE_MATRIX = 0.005
RATE_VECTOR = 0.2
DECAY = 0.1
LANES = 128


def from_behind(value, axis, steps):
    count = lax.axis_size(axis)
    first, last = (max(0, -steps), min(count, count - steps))
    return lax.ppermute(value, axis, [(source, source + steps) for source in range(first, last)])


def matmul(left, right):
    return jnp.dot(left, right, preferred_element_type=jnp.float32)


def matmul_tn(left, right):
    return lax.dot_general(
        left, right, (((0,), (0,)), ((), ())), preferred_element_type=jnp.float32
    )


def matmul_nt(left, right):
    return lax.dot_general(
        left, right, (((1,), (1,)), ((), ())), preferred_element_type=jnp.float32
    )


def inverse_rms(values):
    return lax.rsqrt(jnp.mean(values * values, axis=-1, keepdims=True) + NORM_EPS)


def norm_backward(values, scale, gain, grad_normed):
    weighted = grad_normed * gain
    grad_gain = jnp.sum(grad_normed * values * scale, axis=0)
    cubed = scale * scale * scale
    grad_values = scale * weighted - values * cubed * jnp.mean(
        weighted * values, axis=-1, keepdims=True
    )
    return (grad_values, grad_gain)


def adamw_update(param, grad, first, second, rate, decay):
    first_new = BETA_ONE * first + (1.0 - BETA_ONE) * grad
    second_new = BETA_TWO * second + (1.0 - BETA_TWO) * grad * grad
    first_hat = first_new / (1.0 - BETA_ONE**STEP)
    second_hat = second_new / (1.0 - BETA_TWO**STEP)
    param_new = param - rate * (first_hat / (jnp.sqrt(second_hat) + ADAM_EPS) + decay * param)
    return (param_new, first_new, second_new)


def local(
    hidden_in,
    cotangent,
    doc_position,
    norm_gains,
    conv_taps,
    in_proj,
    out_proj,
    gate_up,
    down_proj,
    first_gains,
    first_taps,
    first_in,
    first_out,
    first_gate_up,
    first_down,
    second_gains,
    second_taps,
    second_in,
    second_out,
    second_gate_up,
    second_down,
):
    half = jnp.bfloat16
    single = jnp.float32
    row_count, length, width = hidden_in.shape
    tok_count = row_count * length
    axes = ("seq", "fsdp")
    in_width = in_proj.shape[1]
    out_width = out_proj.shape[1]
    vectors = jnp.concatenate([norm_gains, conv_taps], axis=0).T.astype(half)
    packed = jnp.concatenate(
        [
            in_proj.astype(half),
            out_proj.astype(half),
            jnp.pad(vectors, ((0, 0), (0, LANES - vectors.shape[1]))),
        ],
        axis=1,
    )
    packed_full = lax.all_gather(packed, axes, axis=0, tiled=True)
    in_full = packed_full[:, :in_width]
    out_full = packed_full[:, in_width : in_width + out_width]
    vectors_full = packed_full[:, in_width + out_width :].astype(single).T
    mixer_full = (None, None, in_full, out_full)
    gains_f = vectors_full[:2]
    taps_f = vectors_full[2:5]
    resid_one = hidden_in.reshape(tok_count, width).astype(single)
    scale_one = inverse_rms(resid_one)
    normed_one = (resid_one * scale_one * gains_f[0]).astype(half)
    projected = matmul(normed_one, mixer_full[2])
    b_branch = projected[:, :width]
    c_branch = projected[:, width : 2 * width]
    x_branch = projected[:, 2 * width :]
    gated_input = (b_branch * x_branch).astype(half)
    gated_rows = gated_input.reshape(row_count, length, width)
    carried = from_behind(gated_rows[:, length - 2 :, :], "seq", 1)
    extended = jnp.concatenate([carried, gated_rows], axis=1).astype(single)
    gated_f = extended[:, 2:].reshape(tok_count, width)
    prev_one = extended[:, 1 : length + 1].reshape(tok_count, width)
    prev_two = extended[:, :length].reshape(tok_count, width)
    positions = doc_position.reshape(tok_count)
    mask_one = (positions >= 1).astype(single)[:, None]
    mask_two = (positions >= 2).astype(single)[:, None]
    conv_out = (
        taps_f[0] * gated_f + mask_one * taps_f[1] * prev_one + mask_two * taps_f[2] * prev_two
    )
    mixer_act = (c_branch * conv_out).astype(half)
    resid_two = resid_one + matmul(mixer_act, mixer_full[3])
    scale_two = inverse_rms(resid_two)
    normed_two = (resid_two * scale_two * gains_f[1]).astype(half)
    ffn_full = (
        lax.all_gather(gate_up.astype(half), ("seq", "fsdp"), axis=0, tiled=True),
        lax.all_gather(down_proj.astype(half), ("seq", "fsdp"), axis=0, tiled=True),
    )
    hidden_units = ffn_full[0].shape[1] // 2
    ffn_pre = matmul(normed_two, ffn_full[0])
    gate_pre = ffn_pre[:, :hidden_units]
    up_pre = ffn_pre[:, hidden_units:]
    sigmoid_gate = jax.nn.sigmoid(gate_pre)
    silu_gate = gate_pre * sigmoid_gate
    ffn_act = (silu_gate * up_pre).astype(half)
    block_out = resid_two + matmul(ffn_act, ffn_full[1])
    cot_rows = cotangent.reshape(tok_count, width)
    grad_act = matmul_nt(cot_rows, ffn_full[1])
    grad_gate = grad_act * up_pre * sigmoid_gate * (1.0 + gate_pre * (1.0 - sigmoid_gate))
    grad_both = jnp.concatenate([grad_gate, grad_act * silu_gate], axis=1).astype(half)
    grad_normed = matmul_nt(grad_both, ffn_full[0])
    grad_down = matmul_tn(ffn_act, cot_rows)
    grad_gate_up = matmul_tn(normed_two, grad_both)
    norm_part, gain_two_grad = norm_backward(resid_two, scale_two, gains_f[1], grad_normed)
    grad_resid = cot_rows.astype(single) + norm_part
    resid_cast = grad_resid.astype(half)
    grad_mixer = matmul_nt(resid_cast, mixer_full[3])
    grad_cbranch = grad_mixer * conv_out
    grad_conv = grad_mixer * c_branch
    masked_one = mask_one * grad_conv
    masked_two = mask_two * grad_conv
    grad_taps = jnp.stack(
        [
            jnp.sum(grad_conv * gated_f, axis=0),
            jnp.sum(masked_one * prev_one, axis=0),
            jnp.sum(masked_two * prev_two, axis=0),
        ]
    )
    one_rows = masked_one.reshape(row_count, length, width)
    two_rows = masked_two.reshape(row_count, length, width)
    leading = from_behind((one_rows[:, :2, :], two_rows[:, :2, :]), "seq", -1)
    ext_one = jnp.concatenate([one_rows, leading[0]], axis=1)
    ext_two = jnp.concatenate([two_rows, leading[1]], axis=1)
    next_one = ext_one[:, 1 : length + 1].reshape(tok_count, width)
    next_two = ext_two[:, 2 : length + 2].reshape(tok_count, width)
    grad_gated = taps_f[0] * grad_conv + taps_f[1] * next_one + taps_f[2] * next_two
    grad_proj = jnp.concatenate(
        [grad_gated * x_branch, grad_cbranch, grad_gated * b_branch], axis=1
    ).astype(half)
    grad_normone = matmul_nt(grad_proj, mixer_full[2])
    first_part, gain_one_grad = norm_backward(resid_one, scale_one, gains_f[0], grad_normone)
    grad_hidden = grad_resid + first_part
    grad_gains = jnp.stack([gain_one_grad, gain_two_grad])
    grad_in = matmul_tn(normed_one, grad_proj)
    grad_out = matmul_tn(mixer_act, resid_cast)
    vector_grads = jnp.concatenate([grad_gains, grad_taps], axis=0)
    vector_count = vector_grads.shape[0]
    grad_sent = jnp.concatenate(
        [
            grad_gate_up.astype(half),
            grad_down.astype(half).reshape(width, -1),
            grad_in.astype(half),
            grad_out.astype(half),
            jnp.pad(vector_grads.T, ((0, 0), (0, LANES - vector_count))).astype(half),
        ],
        axis=1,
    )
    grad_owned = lax.psum_scatter(grad_sent, axes, scatter_dimension=0, tiled=True).astype(single)
    ends = [grad_gate_up.shape[1]]
    for columns in (grad_down.size // width, in_width, out_width):
        ends.append(ends[-1] + columns)
    vector_owned = grad_owned[:, ends[3] : ends[3] + vector_count].T
    owned = (
        vector_owned[:2],
        vector_owned[2:],
        grad_owned[:, ends[1] : ends[2]],
        grad_owned[:, ends[2] : ends[3]],
        grad_owned[:, : ends[0]],
        grad_owned[:, ends[0] : ends[1]].reshape(down_proj.shape),
    )
    params = (norm_gains, conv_taps, in_proj, out_proj, gate_up, down_proj)
    firsts = (first_gains, first_taps, first_in, first_out, first_gate_up, first_down)
    seconds = (second_gains, second_taps, second_in, second_out, second_gate_up, second_down)
    rates = (RATE_VECTOR, RATE_VECTOR, RATE_MATRIX, RATE_MATRIX, RATE_MATRIX, RATE_MATRIX)
    decays = (0.0, 0.0, DECAY, DECAY, DECAY, DECAY)
    updated = [
        adamw_update(
            params[index], owned[index], firsts[index], seconds[index], rates[index], decays[index]
        )
        for index in range(6)
    ]
    out_rows = block_out.reshape(row_count, length, width)
    grad_rows = grad_hidden.reshape(row_count, length, width)
    return (
        out_rows,
        grad_rows,
        owned[0],
        owned[1],
        owned[2],
        owned[3],
        owned[4],
        owned[5],
        updated[0][0],
        updated[1][0],
        updated[2][0],
        updated[3][0],
        updated[4][0],
        updated[5][0],
        updated[0][1],
        updated[1][1],
        updated[2][1],
        updated[3][1],
        updated[4][1],
        updated[5][1],
        updated[0][2],
        updated[1][2],
        updated[2][2],
        updated[3][2],
        updated[4][2],
        updated[5][2],
    )


def solution(mesh):
    in_specs = (
        P("fsdp", "seq", None),
        P("fsdp", "seq", None),
        P("fsdp", "seq"),
        P(None, ("seq", "fsdp")),
        P(None, ("seq", "fsdp")),
        P(("seq", "fsdp"), None),
        P(("seq", "fsdp"), None),
        P(("seq", "fsdp"), None),
        P(("seq", "fsdp"), None),
        P(None, ("seq", "fsdp")),
        P(None, ("seq", "fsdp")),
        P(("seq", "fsdp"), None),
        P(("seq", "fsdp"), None),
        P(("seq", "fsdp"), None),
        P(("seq", "fsdp"), None),
        P(None, ("seq", "fsdp")),
        P(None, ("seq", "fsdp")),
        P(("seq", "fsdp"), None),
        P(("seq", "fsdp"), None),
        P(("seq", "fsdp"), None),
        P(("seq", "fsdp"), None),
    )
    out_specs = (
        P("fsdp", "seq", None),
        P("fsdp", "seq", None),
        P(None, ("seq", "fsdp")),
        P(None, ("seq", "fsdp")),
        P(("seq", "fsdp"), None),
        P(("seq", "fsdp"), None),
        P(("seq", "fsdp"), None),
        P(("seq", "fsdp"), None),
        P(None, ("seq", "fsdp")),
        P(None, ("seq", "fsdp")),
        P(("seq", "fsdp"), None),
        P(("seq", "fsdp"), None),
        P(("seq", "fsdp"), None),
        P(("seq", "fsdp"), None),
        P(None, ("seq", "fsdp")),
        P(None, ("seq", "fsdp")),
        P(("seq", "fsdp"), None),
        P(("seq", "fsdp"), None),
        P(("seq", "fsdp"), None),
        P(("seq", "fsdp"), None),
        P(None, ("seq", "fsdp")),
        P(None, ("seq", "fsdp")),
        P(("seq", "fsdp"), None),
        P(("seq", "fsdp"), None),
        P(("seq", "fsdp"), None),
        P(("seq", "fsdp"), None),
    )
    return jax.shard_map(local, mesh=mesh, in_specs=in_specs, out_specs=out_specs, check_vma=False)
```
